32 devices in a mesh: gx: 16 (over z, x, core), gy: 2 (over y).
Axes of the slice: x: 2, y: 2, z: 4, core: 2. Of those that a mesh axis runs over, the one named last changes fastest.
Arguments:
- queries: bfloat16 [64, 128, 1024], P('gx', 'gy'), may hold values from -42 to 42
- key_tokens: bfloat16 [64, 128, 1024], P('gx', 'gy'), may hold values from -6 to 6
- value_tokens: bfloat16 [64, 128, 1024], P('gx', 'gy'), may hold values from -6 to 6
- out_grad: bfloat16 [64, 128, 1024], P('gx', 'gy'), may hold values from -6 to 6
- conv_weight: float32 [9, 1024], replicated, may hold values from -0.9 to 0.9
- block_pairs: int32 [16, 2, 16, 2], P('gx', 'gy'), may hold values from 0 to 31, as said below
Outputs:
- layer_out: bfloat16 [64, 128, 1024], P('gx', 'gy')
- query_grad: bfloat16 [64, 128, 1024], P('gx', 'gy')
- key_grad: bfloat16 [64, 128, 1024], P('gx', 'gy')
- value_grad: bfloat16 [64, 128, 1024], P('gx', 'gy')
The draws below stay inside these ranges and needn't reach their ends.
Inputs may be any that keep to these rules, and one draw needn't show every extreme that they name: block_pairs[i, j, p] = (a local query block of tile (i, j), below 2; a key block of column j, which lies on tile (key block) // 2 along the first dimension). That tile is i + o modulo 16 with o one of 0, 1, -1, 4, 8, 12. Pairs may repeat.
All inputs are finite; a program needn't handle non-finite values.
Results may differ from the reference program's by a relative error of at most 0.009.
Values may be sent and summed in bfloat16 or wider, within the bound.
A program may use at most 128 MiB of HBM per device.

```python
import math
import jax
import jax.numpy as jnp
from jax import lax

H = 8
HD = 128
TX = 4
TY = 64
BLOCK = 128
PAIRS = 16
C = 1024
TILES_X = 16
TILES_Y = 2
STRIDE = 4
QB = 2
KBLK = 32
GRID_X = 64
GRID_Y = 128


def common_draw(base_key):
    key_query = jax.random.fold_in(base_key, 11)
    key_keys = jax.random.fold_in(base_key, 12)
    shape_all = (GRID_X, GRID_Y, H * HD)
    query_values = 2.0 * jnp.clip(jax.random.normal(key_query, shape_all, jnp.float32), -6.0, 6.0)
    key_values = jnp.clip(jax.random.normal(key_keys, shape_all, jnp.float32), -6.0, 6.0)
    return (query_values, key_values)


def draw_queries(key, part):
    return common_draw(key)[0].astype(jnp.bfloat16)


def draw_key_tokens(key, part):
    return common_draw(key)[1].astype(jnp.bfloat16)


def draw_block_pairs(key, part):
    key_count = jax.random.fold_in(key, 21)
    key_qblock = jax.random.fold_in(key, 22)
    key_pick = jax.random.fold_in(key, 23)
    key_local = jax.random.fold_in(key, 24)
    shape_pairs = (TILES_X, TILES_Y, PAIRS)
    live_count = jax.random.randint(key_count, (TILES_X, TILES_Y, 1), 2, PAIRS + 1)
    query_block = jax.random.randint(key_qblock, shape_pairs, 0, QB)
    offset_pick = jax.random.randint(key_pick, shape_pairs, 0, 6)
    local_block = jax.random.randint(key_local, shape_pairs, 0, QB)
    offset_table = jnp.array([0, 1, TILES_X - 1, STRIDE, 2 * STRIDE, 3 * STRIDE], dtype=jnp.int32)
    offset_values = offset_table[offset_pick]
    tile_ids = jnp.arange(TILES_X, dtype=jnp.int32).reshape(TILES_X, 1, 1)
    owner_tile = (tile_ids + offset_values) % TILES_X
    key_block = owner_tile * QB + local_block
    pair_index = jnp.arange(PAIRS, dtype=jnp.int32).reshape(1, 1, PAIRS)
    self_block = tile_ids * QB + query_block
    key_block = jnp.where(pair_index < live_count, key_block, self_block)
    first_query = jnp.full(shape_pairs, QB - 1, jnp.int32)
    first_key = (tile_ids + TILES_X - 1) % TILES_X * QB + QB - 1 + jnp.zeros(shape_pairs, jnp.int32)
    second_key = tile_ids * QB + jnp.zeros(shape_pairs, jnp.int32)
    query_block = jnp.where(pair_index == 0, first_query, jnp.where(pair_index == 1, 0, query_block))
    key_block = jnp.where(pair_index == 0, first_key, jnp.where(pair_index == 1, second_key, key_block))
    return jnp.stack((query_block, key_block), axis=3)


def shard_levels(rng, shape, split, smallest, high):
    factor_of = 1.0
    for axis_at, shards_of in split:
        heights = jax.random.uniform(jax.random.fold_in(jax.random.fold_in(rng, 6), axis_at), (shards_of,), jnp.float32, smallest / len(split), high / len(split))
        factor_of = factor_of * jnp.repeat(jnp.exp(heights), shape[axis_at] // shards_of).reshape((-1,) + (1,) * (len(shape) - 1 - axis_at))
    return factor_of


def bell_draw(own_key, shape, width, bound, shards=(), kind=jnp.bfloat16):
    values = jax.random.normal(own_key, shape, jnp.float32) * width
    if len(shards) > 0:
        values = shard_levels(own_key, shape, shards, -0.22, 0.18) * values
    return jnp.clip(values, min=-bound, max=bound).astype(kind)


def setup_inputs(seed: int = 0) -> dict:
    keys = jax.random.split(jax.random.key(seed), 7)
    queries = draw_queries(jax.random.fold_in(keys[6], 71), 0)
    key_tokens = draw_key_tokens(jax.random.fold_in(keys[6], 71), 0)
    value_tokens = bell_draw(keys[2], (GRID_X, GRID_Y, C), 1.0, 6.0, ((0, 16), (1, 2)))
    out_grad = bell_draw(keys[3], (GRID_X, GRID_Y, C), 1.0, 6.0, ((0, 16), (1, 2)))
    conv_weight = bell_draw(keys[4], (9, C), 0.15, 0.9, (), jnp.float32)
    block_pairs = draw_block_pairs(jax.random.fold_in(keys[6], 71), 0)
    return {"queries": queries, "key_tokens": key_tokens, "value_tokens": value_tokens, "out_grad": out_grad, "conv_weight": conv_weight, "block_pairs": block_pairs}


lowest_score = -1e+30

def stencil(padded, weights, direction, row_count, col_count):
    running_sum = jnp.zeros((row_count, col_count, padded.shape[2]), jnp.float32)
    for row_step in (-1, 0, 1):
        for col_step in (-1, 0, 1):
            row_first = 1 + direction * row_step
            col_first = 1 + direction * col_step
            window = padded[row_first:row_first + row_count, col_first:col_first + col_count]
            running_sum = running_sum + weights[3 * (row_step + 1) + col_step + 1] * window
    return running_sum

def reference(queries, key_tokens, value_tokens, out_grad, conv_weight, block_pairs):
    scale_factor = 1.0 / math.sqrt(HD)
    token_count = TX * TY
    offsets = jnp.array([0, 1, TILES_X - 1, STRIDE, 2 * STRIDE, 3 * STRIDE], dtype=jnp.int32)
    value_pad = jnp.pad(value_tokens.astype(jnp.float32), ((1, 1), (1, 1), (0, 0)))
    grad_pad = jnp.pad(out_grad.astype(jnp.float32), ((1, 1), (1, 1), (0, 0)))
    conv_value = stencil(value_pad, conv_weight, 1, GRID_X, GRID_Y)
    conv_back = stencil(grad_pad, conv_weight, -1, GRID_X, GRID_Y)

    def column(column_index):
        first_y = column_index * TY

        def column_strip(array):
            return lax.dynamic_slice_in_dim(array, first_y, TY, 1).reshape(TILES_X, token_count, H, HD)
        query_strip = column_strip(queries)
        key_strip = column_strip(key_tokens)
        value_strip = column_strip(value_tokens)
        grad_strip = column_strip(out_grad)
        pair_strip = lax.dynamic_index_in_dim(block_pairs, column_index, 1, keepdims=False)
        tile_ids = jnp.arange(TILES_X, dtype=jnp.int32)
        query_global = (tile_ids[:, None] * QB + pair_strip[:, :, 0]).reshape(-1)
        key_global = pair_strip[:, :, 1].reshape(-1)
        every_block = jnp.arange(KBLK, dtype=jnp.int32)
        query_onehot = (query_global[:, None] == every_block[None, :]).astype(jnp.float32)
        key_onehot = (key_global[:, None] == every_block[None, :]).astype(jnp.float32)
        counts = jnp.dot(query_onehot.T, key_onehot, precision=lax.Precision.HIGHEST, preferred_element_type=jnp.float32)
        block_allow = (counts > 0.5) | (every_block[:, None] == every_block[None, :])

        def tile_step(totals, tile_index):
            key_acc, value_acc = totals
            near_tiles = (tile_index + offsets) % TILES_X
            key_near = key_strip[near_tiles].reshape(6 * token_count, H, HD).astype(jnp.float32)
            value_near = value_strip[near_tiles].reshape(6 * token_count, H, HD).astype(jnp.float32)
            row_allow = lax.dynamic_slice_in_dim(block_allow, tile_index * QB, QB, 0)
            columns = (near_tiles[:, None] * QB + jnp.arange(QB, dtype=jnp.int32)[None, :]).reshape(-1)
            allowed = row_allow[:, columns]
            query_tile = lax.dynamic_index_in_dim(query_strip, tile_index, 0, keepdims=False).astype(jnp.float32)
            grad_tile = lax.dynamic_index_in_dim(grad_strip, tile_index, 0, keepdims=False).astype(jnp.float32)
            scores = jnp.einsum('qhd,khd->hqk', query_tile, key_near) * scale_factor
            shaped = (H, QB, BLOCK, 6 * QB, BLOCK)
            visible = jnp.broadcast_to(allowed[None, :, None, :, None], shaped).reshape(H, token_count, 6 * token_count)
            row_max = lax.optimization_barrier(jnp.max(jnp.where(visible, scores, lowest_score), axis=2))
            log_total = row_max + jnp.log(lax.optimization_barrier(jnp.sum(jnp.where(visible, jnp.exp(scores - row_max[:, :, None]), 0.0), axis=2)))
            probabilities = jnp.where(visible, jnp.exp(scores - log_total[:, :, None]), 0.0)
            weights = probabilities.astype(jnp.bfloat16).astype(jnp.float32)
            attended = jnp.einsum('hqk,khd->qhd', weights, value_near)
            grad_dot = jnp.einsum('qhd,qhd->hq', grad_tile, attended)
            prob_grad = jnp.einsum('qhd,khd->hqk', grad_tile, value_near)
            score_grad = (probabilities * (prob_grad - grad_dot[:, :, None]) * scale_factor).astype(jnp.bfloat16).astype(jnp.float32)
            dquery = jnp.einsum('hqk,khd->qhd', score_grad, key_near)
            key_part = jnp.einsum('hqk,qhd->khd', score_grad, query_tile).reshape(6, token_count, H, HD)
            value_part = jnp.einsum('hqk,qhd->khd', weights, grad_tile).reshape(6, token_count, H, HD)
            key_acc = key_acc.at[near_tiles].add(key_part)
            value_acc = value_acc.at[near_tiles].add(value_part)
            return ((key_acc, value_acc), (attended, dquery))
        zeros_acc = jnp.zeros((TILES_X, token_count, H, HD), jnp.float32)
        (key_acc, value_acc), (attended_all, dquery_all) = lax.scan(tile_step, (zeros_acc, zeros_acc), jnp.arange(TILES_X, dtype=jnp.int32))

        def to_grid(array):
            return array.reshape(GRID_X, TY, H * HD)
        return (to_grid(attended_all), to_grid(dquery_all), to_grid(key_acc), to_grid(value_acc))
    stacked = lax.map(column, jnp.arange(TILES_Y, dtype=jnp.int32))

    def assemble(array):
        return jnp.moveaxis(array, 0, 1).reshape(GRID_X, GRID_Y, H * HD)
    attended = assemble(stacked[0])
    dquery = assemble(stacked[1])
    dkey = assemble(stacked[2])
    dvalue = assemble(stacked[3])
    layer_out = (attended + conv_value).astype(jnp.bfloat16)
    value_grad = (dvalue + conv_back).astype(jnp.bfloat16)
    return (layer_out, dquery.astype(jnp.bfloat16), dkey.astype(jnp.bfloat16), value_grad)
```

```python
import functools
import math

import jax
import jax.numpy as jnp
from jax import lax
from jax.experimental import pallas as pl
from jax.experimental.pallas import tpu as pltpu
from jax.sharding import PartitionSpec as P

HD = 128
BLOCK = 128
NEG = -1e30
MESH = pl.DeviceIdType.MESH
SCALE = 1.0 / math.sqrt(HD)
LOG2E = math.log2(math.e)
F32 = jnp.float32
BF16 = jnp.bfloat16


def kernel(
    n, m, tx, ty,
    q_ref, k_ref, v_ref, g_ref, w_ref, bias_ref,
    o_ref, dq_ref, dk_ref, dv_ref,
    qg, gg, kk, vv, bias_g, s_sc, dk_acc, dv_acc,
    part_send, part_recv, res, ret, edge, slab, conv,
    send_sem, recv_sem, local_sem,
):
    tokens = tx * ty
    heads = q_ref.shape[2] // HD
    hp = heads // 4
    quarter = n // 4
    own = lax.axis_index("gx")
    col = lax.axis_index("gy")
    slot = own // quarter
    rank = lax.rem(own, quarter)

    def far(d):
        return {"gx": lax.rem(own + d * quarter, n)}

    next_group = {"gx": slot * quarter + lax.rem(rank + 1, quarter)}
    prev_group = {"gx": slot * quarter + lax.rem(rank + quarter - 1, quarter)}
    next_tile = {"gx": lax.rem(own + 1, n)}
    prev_tile = {"gx": lax.rem(own + n - 1, n)}
    next_col = {"gy": lax.rem(col + 1, m)}
    prev_col = {"gy": lax.rem(col + m - 1, m)}

    barrier = pltpu.get_barrier_semaphore()
    partners = [far(1), far(2), far(3), next_group, prev_group, next_tile, prev_tile, next_col, prev_col]
    for partner in partners:
        pl.semaphore_signal(barrier, inc=1, device_id=partner, device_id_type=MESH)
    pl.semaphore_wait(barrier, len(partners))

    count = [0]
    sent = []

    def send(src, dst, device):
        at = count[0]
        count[0] += 1
        copy = pltpu.make_async_remote_copy(
            src_ref=src, dst_ref=dst, send_sem=send_sem.at[at], recv_sem=recv_sem.at[at],
            device_id=device, device_id_type=MESH,
        )
        copy.start()
        sent.append(copy)
        return copy

    def head_cols(head):
        return pl.ds(pl.multiple_of(head * HD, HD), HD)

    order = (2, 1, 3)
    arrays = ((k_ref, lambda h, s: kk.at[h, 0, s]), (v_ref, lambda h, s: vv.at[h, 0, s]),
              (q_ref, lambda h, s: qg.at[h, s]), (g_ref, lambda h, s: gg.at[h, s]))
    edge_copies = []
    for a, ref in enumerate((v_ref, g_ref)):
        edge_copies.append(send(ref.at[pl.ds(tx - 1, 1)], edge.at[a, pl.ds(0, 1)], next_tile))
        edge_copies.append(send(ref.at[pl.ds(0, 1)], edge.at[a, pl.ds(1, 1)], prev_tile))
    incoming = {}
    locals_ = []
    for h in range(hp):
        for a, (ref, place) in enumerate(arrays):
            for d in order:
                target = lax.rem(slot + d, 4)
                incoming[h, a, d] = send(ref.at[:, :, head_cols(target * hp + h)], place(h, slot), far(d))
            mine = pltpu.make_async_copy(
                ref.at[:, :, head_cols(slot * hp + h)], place(h, slot), local_sem.at[h * 4 + a])
            mine.start()
            locals_.append(mine)
        if h == 0:
            bias_copies = [send(bias_ref, bias_g.at[slot], far(d)) for d in order]
            mine = pltpu.make_async_copy(bias_ref, bias_g.at[slot], local_sem.at[hp * 4])
            mine.start()
            locals_.append(mine)
    slab_copies = []
    for a, ref in enumerate((v_ref, g_ref)):
        slab_copies.append(send(ref.at[:, pl.ds(ty - 16, 16)], slab.at[a, 0, pl.ds(1, tx)], next_col))
        slab_copies.append(send(ref.at[:, pl.ds(0, 16)], slab.at[a, 1, pl.ds(1, tx)], prev_col))
    for mine in locals_:
        mine.wait()

    forwards = {}

    def forward(h, d):
        s = lax.rem(slot + 4 - d, 4)
        for a, buf in enumerate((kk, vv)):
            if d:
                incoming[h, a, d].wait_recv()
            forwards[h, a, d, 1] = send(buf.at[h, 0, s], buf.at[h, 1, s], prev_group)
            forwards[h, a, d, 2] = send(buf.at[h, 0, s], buf.at[h, 2, s], next_group)

    for h in range(hp):
        forward(h, 0)
    for copy in edge_copies:
        copy.wait_recv()
    for a in range(2):
        for x, e in ((0, 0), (tx + 1, 1)):
            slab_copies.append(send(edge.at[a, pl.ds(e, 1), pl.ds(ty - 16, 16)], slab.at[a, 0, pl.ds(x, 1)], next_col))
            slab_copies.append(send(edge.at[a, pl.ds(e, 1), pl.ds(0, 16)], slab.at[a, 1, pl.ds(x, 1)], prev_col))
    for d in (1, 3, 2):
        forward(0, d)

    for copy in slab_copies:
        copy.wait_recv()
    has_up = (own > 0).astype(F32)
    has_down = (own < n - 1).astype(F32)
    has_left = (col > 0).astype(F32)
    has_right = (col < m - 1).astype(F32)
    for a, ref in enumerate((v_ref, g_ref)):

        @pl.loop(0, heads)
        def _(c, a=a, ref=ref):
            cols = head_cols(c)
            row_id = lax.broadcasted_iota(jnp.int32, (ty, HD), 0)
            sums = [None] * tx
            for x in range(tx + 2):
                if x == 0:
                    row = edge[a, 0, :, cols].astype(F32) * has_up
                elif x == tx + 1:
                    row = edge[a, 1, :, cols].astype(F32) * has_down
                else:
                    row = ref[x - 1, :, cols].astype(F32)
                left = slab[a, 0, x, :, cols].astype(F32)[15:16] * has_left
                right = slab[a, 1, x, :, cols].astype(F32)[0:1] * has_right
                if x == 0:
                    left, right = left * has_up, right * has_up
                if x == tx + 1:
                    left, right = left * has_down, right * has_down
                shifted = (
                    jnp.where(row_id == 0, left, pltpu.roll(row, 1, 0)),
                    row,
                    jnp.where(row_id == ty - 1, right, pltpu.roll(row, ty - 1, 0)),
                )
                for step in (-1, 0, 1):
                    target = x - 1 - step
                    if 0 <= target < tx:
                        for b in range(3):
                            tap = 3 * (step + 1) + b
                            tap = tap if a == 0 else 8 - tap
                            term = w_ref[pl.ds(tap, 1), cols] * shifted[b]
                            sums[target] = term if sums[target] is None else sums[target] + term
            for x in range(tx):
                conv[a, x, :, cols] = sums[x]

    for h in range(1, hp):
        for d in (1, 3, 2):
            forward(h, d)
    for copy in bias_copies:
        copy.wait_recv()

    ahead = (rank == quarter - 1).astype(jnp.int32)
    behind = 3 * (rank == 0).astype(jnp.int32)
    nt = (((1,), (1,)), ((), ()))
    nn = (((1,), (0,)), ((), ()))
    tn = (((0,), (0,)), ((), ()))

    def dot(x, y, dims):
        return lax.dot_general(x, y, dims, preferred_element_type=F32)

    def flat(x):
        return x.reshape(tokens, HD)

    def attend(h):
        dk_acc[h] = jnp.zeros(dk_acc.shape[1:], F32)
        dv_acc[h] = jnp.zeros(dv_acc.shape[1:], F32)

        @pl.loop(0, 4)
        def _(i):
            q = flat(qg[h, i])
            g = flat(gg[h, i])
            keys = [(0, 0), (0, 1), (0, 2), (0, 3), (1, lax.rem(i + ahead, 4)), (2, lax.rem(i + behind, 4))]
            top = None
            for j, (nb, s) in enumerate(keys):
                js = pl.ds(j * tokens, tokens)
                score = dot(q, flat(kk[h, nb, s]), nt)
                bias = bias_g[i, :, js]
                parts = [score[b * BLOCK:(b + 1) * BLOCK] + bias[b:b + 1] for b in range(tokens // BLOCK)]
                score = jnp.concatenate(parts, axis=0)
                s_sc[:, js] = score
                peak = jnp.max(score, axis=1, keepdims=True)
                top = peak if top is None else jnp.maximum(top, peak)
            total = jnp.zeros((tokens, 1), F32)
            out = jnp.zeros((tokens, HD), F32)
            for j, (nb, s) in enumerate(keys):
                js = pl.ds(j * tokens, tokens)
                prob = jnp.exp2((s_sc[:, js] - top) * (SCALE * LOG2E))
                s_sc[:, js] = prob
                total = total + jnp.sum(prob, axis=1, keepdims=True)
                out = out + dot(prob.astype(BF16), flat(vv[h, nb, s]), nn)
            inv = 1.0 / total
            out = out * inv
            res[0, h, i] = out.astype(BF16).reshape(tx, ty, HD)
            grad_dot = jnp.sum(g.astype(F32) * out, axis=1, keepdims=True)
            dq = jnp.zeros((tokens, HD), F32)
            for j, (nb, s) in enumerate(keys):
                js = pl.ds(j * tokens, tokens)
                prob_grad = dot(g, flat(vv[h, nb, s]), nt)
                prob = s_sc[:, js] * inv
                score_grad = (prob * (prob_grad - grad_dot)).astype(BF16)
                dq = dq + dot(score_grad, flat(kk[h, nb, s]), nn)
                dk = dot(score_grad, q, tn)
                dv = dot(prob.astype(BF16), g, tn)
                if nb == 0:
                    dk_acc[h, s] += dk
                    dv_acc[h, s] += dv
                else:
                    part_send[0, h, nb - 1, s] = dk.astype(BF16).reshape(tx, ty, HD)
                    part_send[1, h, nb - 1, s] = dv.astype(BF16).reshape(tx, ty, HD)
            res[1, h, i] = (dq * SCALE).astype(BF16).reshape(tx, ty, HD)

    back = []

    def give_back(a, h):
        for d in order:
            target = lax.rem(slot + d, 4)
            back.append(send(res.at[a, h, target], ret.at[a, slot * hp + h], far(d)))

    parts = {}

    def work(h):
        for d in order:
            for a in (2, 3):
                incoming[h, a, d].wait_recv()
        for a in range(2):
            for d in range(4):
                for nb in (1, 2):
                    forwards[h, a, d, nb].wait_recv()
        attend(h)
        parts[h] = [
            send(part_send.at[a, h, nb], part_recv.at[a, h, nb], (next_group, prev_group)[nb])
            for a in range(2) for nb in range(2)
        ]
        for a in (0, 1):
            give_back(a, h)

    def finish(h):
        for copy in parts[h]:
            copy.wait_recv()
        for a, acc in enumerate((dk_acc, dv_acc)):
            for s in range(4):
                value = acc[h, s] + flat(part_recv[a, h, 0, s]).astype(F32) + flat(part_recv[a, h, 1, s]).astype(F32)
                if a == 0:
                    value = value * SCALE
                res[2 + a, h, s] = value.astype(BF16).reshape(tx, ty, HD)
            give_back(2 + a, h)

    for h in range(hp):
        work(h)
    for h in range(hp):
        finish(h)
    for a in range(4):
        for h in range(hp):
            ret[a, slot * hp + h] = res[a, h, slot]
    for copy in back:
        copy.wait_recv()
    for c in range(heads):
        cols = pl.ds(c * HD, HD)
        o_ref[:, :, cols] = (ret[0, c].astype(F32) + conv[0, :, :, cols]).astype(BF16)
        dq_ref[:, :, cols] = ret[1, c]
        dk_ref[:, :, cols] = ret[2, c]
        dv_ref[:, :, cols] = (ret[3, c].astype(F32) + conv[1, :, :, cols]).astype(BF16)
    for copy in sent:
        copy.wait_send()


def bias_rows(block_pairs, n, tokens):
    quarter = n // 4
    own = lax.axis_index("gx")
    rank = own % quarter
    blocks = tokens // BLOCK
    tiles = jnp.concatenate([
        rank + quarter * jnp.arange(4, dtype=jnp.int32),
        jnp.stack([(own + 1) % n, (own + n - 1) % n]).astype(jnp.int32),
    ])
    key_at = jnp.repeat(tiles, tokens) * blocks + jnp.tile(jnp.arange(tokens, dtype=jnp.int32) // BLOCK, 6)
    query = jnp.arange(8, dtype=jnp.int32)
    pairs = block_pairs[0, 0]
    listed = (pairs[:, 0][:, None, None] == query[None, :, None]) & (pairs[:, 1][:, None, None] == key_at[None, None, :])
    allowed = jnp.any(listed, axis=0) | ((own * blocks + query)[:, None] == key_at[None, :])
    return jnp.where(allowed, 0.0, NEG).astype(F32)


def per_device(n, m, queries, key_tokens, value_tokens, out_grad, conv_weight, block_pairs):
    tx, ty, width = queries.shape
    heads = width // HD
    hp = heads // 4
    tokens = tx * ty
    bias = bias_rows(block_pairs, n, tokens)
    vmem = pl.BlockSpec(memory_space=pltpu.VMEM)
    shape = jax.ShapeDtypeStruct(queries.shape, BF16)
    return pl.pallas_call(
        functools.partial(kernel, n, m, tx, ty),
        out_shape=(shape,) * 4,
        in_specs=[vmem] * 6,
        out_specs=(vmem,) * 4,
        scratch_shapes=[
            pltpu.VMEM((hp, 4, tx, ty, HD), BF16),
            pltpu.VMEM((hp, 4, tx, ty, HD), BF16),
            pltpu.VMEM((hp, 3, 4, tx, ty, HD), BF16),
            pltpu.VMEM((hp, 3, 4, tx, ty, HD), BF16),
            pltpu.VMEM((4, 8, 6 * tokens), F32),
            pltpu.VMEM((tokens, 6 * tokens), F32),
            pltpu.VMEM((hp, 4, tokens, HD), F32),
            pltpu.VMEM((hp, 4, tokens, HD), F32),
            pltpu.VMEM((2, hp, 2, 4, tx, ty, HD), BF16),
            pltpu.VMEM((2, hp, 2, 4, tx, ty, HD), BF16),
            pltpu.VMEM((4, hp, 4, tx, ty, HD), BF16),
            pltpu.VMEM((4, heads, tx, ty, HD), BF16),
            pltpu.VMEM((2, 2, ty, width), BF16),
            pltpu.VMEM((2, 2, tx + 2, 16, width), BF16),
            pltpu.VMEM((2, tx, ty, width), F32),
            pltpu.SemaphoreType.DMA((160,)),
            pltpu.SemaphoreType.DMA((160,)),
            pltpu.SemaphoreType.DMA((4 * hp + 1,)),
        ],
        compiler_params=pltpu.CompilerParams(
            collective_id=0, has_side_effects=True, vmem_limit_bytes=60 * 1024 * 1024
        ),
    )(queries, key_tokens, value_tokens, out_grad, conv_weight, bias)


def solution(mesh):
    grid = P("gx", "gy", None)
    return jax.shard_map(
        functools.partial(per_device, mesh.shape["gx"], mesh.shape["gy"]),
        mesh=mesh,
        in_specs=(grid, grid, grid, grid, P(), P("gx", "gy", None, None)),
        out_specs=(grid, grid, grid, grid),
        check_vma=False,
    )
```

```python
import functools
import math

import jax
import jax.numpy as jnp
from jax import lax
from jax.experimental import pallas as pl
from jax.experimental.pallas import tpu as pltpu
from jax.sharding import PartitionSpec as P

HD = 128
BLOCK = 128
NEG = -1e30
MESH = pl.DeviceIdType.MESH
SCALE = 1.0 / math.sqrt(HD)
LOG2E = math.log2(math.e)
F32 = jnp.float32
BF16 = jnp.bfloat16


def kernel(
    n, m, tx, ty,
    q_ref, k_ref, v_ref, g_ref, w_ref, bias_ref,
    o_ref, dq_ref, dk_ref, dv_ref,
    qg, gg, kk, vv, bias_g, s_sc, dk_acc, dv_acc,
    part_send, part_recv, res, ret, edge, slab, conv,
    send_sem, recv_sem, local_sem,
):
    tokens = tx * ty
    heads = q_ref.shape[2] // HD
    hp = heads // 4
    quarter = n // 4
    own = lax.axis_index("gx")
    col = lax.axis_index("gy")
    slot = own // quarter
    rank = lax.rem(own, quarter)

    def far(d):
        return {"gx": lax.rem(own + d * quarter, n)}

    next_group = {"gx": slot * quarter + lax.rem(rank + 1, quarter)}
    prev_group = {"gx": slot * quarter + lax.rem(rank + quarter - 1, quarter)}
    next_tile = {"gx": lax.rem(own + 1, n)}
    prev_tile = {"gx": lax.rem(own + n - 1, n)}
    next_col = {"gy": lax.rem(col + 1, m)}
    prev_col = {"gy": lax.rem(col + m - 1, m)}

    barrier = pltpu.get_barrier_semaphore()
    partners = [far(1), far(2), far(3), next_group, prev_group, next_tile, prev_tile, next_col, prev_col]
    for partner in partners:
        pl.semaphore_signal(barrier, inc=1, device_id=partner, device_id_type=MESH)
    pl.semaphore_wait(barrier, len(partners))

    count = [0]
    sent = []

    def send(src, dst, device):
        at = count[0]
        count[0] += 1
        copy = pltpu.make_async_remote_copy(
            src_ref=src, dst_ref=dst, send_sem=send_sem.at[at], recv_sem=recv_sem.at[at],
            device_id=device, device_id_type=MESH,
        )
        copy.start()
        sent.append(copy)
        return copy

    edge_copies = []

    def edge_send(src, dst, device, sends, receives):
        at = count[0]
        count[0] += 1
        copy = pltpu.make_async_remote_copy(
            src_ref=src, dst_ref=dst, send_sem=send_sem.at[at], recv_sem=recv_sem.at[at],
            device_id=device, device_id_type=MESH,
        )

        @pl.when(sends)
        def _():
            copy.start()

        @pl.when(jnp.logical_not(receives))
        def _():
            dst[...] = jnp.zeros(dst.shape, BF16)

        edge_copies.append((copy, sends, receives))

    def head_cols(head):
        return pl.ds(pl.multiple_of(head * HD, HD), HD)

    order = (2, 1, 3)
    arrays = ((k_ref, lambda h, s: kk.at[h, 0, s]), (v_ref, lambda h, s: vv.at[h, 0, s]),
              (q_ref, lambda h, s: qg.at[h, s]), (g_ref, lambda h, s: gg.at[h, s]))
    incoming = {}
    locals_ = []
    for h in range(hp):
        for a, (ref, place) in enumerate(arrays):
            for d in order:
                target = lax.rem(slot + d, 4)
                incoming[h, a, d] = send(ref.at[:, :, head_cols(target * hp + h)], place(h, slot), far(d))
            mine = pltpu.make_async_copy(
                ref.at[:, :, head_cols(slot * hp + h)], place(h, slot), local_sem.at[h * 4 + a])
            mine.start()
            locals_.append(mine)
        if h == 0:
            for a, ref in enumerate((v_ref, g_ref)):
                edge_send(ref.at[pl.ds(tx - 1, 1)], edge.at[a, pl.ds(0, 1)], next_tile, own < n - 1, own > 0)
                edge_send(ref.at[pl.ds(0, 1)], edge.at[a, pl.ds(1, 1)], prev_tile, own > 0, own < n - 1)
            bias_copies = [send(bias_ref, bias_g.at[slot], far(d)) for d in order]
            mine = pltpu.make_async_copy(bias_ref, bias_g.at[slot], local_sem.at[hp * 4])
            mine.start()
            locals_.append(mine)
    slab_copies = []
    for a, ref in enumerate((v_ref, g_ref)):
        slab_copies.append(send(ref.at[:, pl.ds(ty - 16, 16)], slab.at[a, 0, pl.ds(1, tx)], next_col))
        slab_copies.append(send(ref.at[:, pl.ds(0, 16)], slab.at[a, 1, pl.ds(1, tx)], prev_col))
    for mine in locals_:
        mine.wait()

    forwards = {}

    def forward(h, d):
        s = lax.rem(slot + 4 - d, 4)
        for a, buf in enumerate((kk, vv)):
            if d:
                incoming[h, a, d].wait_recv()
            forwards[h, a, d, 1] = send(buf.at[h, 0, s], buf.at[h, 1, s], prev_group)
            forwards[h, a, d, 2] = send(buf.at[h, 0, s], buf.at[h, 2, s], next_group)

    for h in range(hp):
        forward(h, 0)
    for copy, _, receives in edge_copies:
        pl.when(receives)(copy.wait_recv)
    for a in range(2):
        for x, e in ((0, 0), (tx + 1, 1)):
            slab_copies.append(send(edge.at[a, pl.ds(e, 1), pl.ds(ty - 16, 16)], slab.at[a, 0, pl.ds(x, 1)], next_col))
            slab_copies.append(send(edge.at[a, pl.ds(e, 1), pl.ds(0, 16)], slab.at[a, 1, pl.ds(x, 1)], prev_col))
    for d in (1, 3, 2):
        forward(0, d)

    for copy in slab_copies:
        copy.wait_recv()
    has_up = (own > 0).astype(F32)
    has_down = (own < n - 1).astype(F32)
    has_left = (col > 0).astype(F32)
    has_right = (col < m - 1).astype(F32)
    for a, ref in enumerate((v_ref, g_ref)):

        @pl.loop(0, heads)
        def _(c, a=a, ref=ref):
            cols = head_cols(c)
            row_id = lax.broadcasted_iota(jnp.int32, (ty, HD), 0)
            sums = [None] * tx
            for x in range(tx + 2):
                if x == 0:
                    row = edge[a, 0, :, cols].astype(F32) * has_up
                elif x == tx + 1:
                    row = edge[a, 1, :, cols].astype(F32) * has_down
                else:
                    row = ref[x - 1, :, cols].astype(F32)
                left = slab[a, 0, x, :, cols].astype(F32)[15:16] * has_left
                right = slab[a, 1, x, :, cols].astype(F32)[0:1] * has_right
                if x == 0:
                    left, right = left * has_up, right * has_up
                if x == tx + 1:
                    left, right = left * has_down, right * has_down
                shifted = (
                    jnp.where(row_id == 0, left, pltpu.roll(row, 1, 0)),
                    row,
                    jnp.where(row_id == ty - 1, right, pltpu.roll(row, ty - 1, 0)),
                )
                for step in (-1, 0, 1):
                    target = x - 1 - step
                    if 0 <= target < tx:
                        for b in range(3):
                            tap = 3 * (step + 1) + b
                            tap = tap if a == 0 else 8 - tap
                            term = w_ref[pl.ds(tap, 1), cols] * shifted[b]
                            sums[target] = term if sums[target] is None else sums[target] + term
            for x in range(tx):
                conv[a, x, :, cols] = sums[x]

    for h in range(1, hp):
        for d in (1, 3, 2):
            forward(h, d)
    for copy in bias_copies:
        copy.wait_recv()

    ahead = (rank == quarter - 1).astype(jnp.int32)
    behind = 3 * (rank == 0).astype(jnp.int32)
    nt = (((1,), (1,)), ((), ()))
    nn = (((1,), (0,)), ((), ()))
    tn = (((0,), (0,)), ((), ()))

    def dot(x, y, dims):
        return lax.dot_general(x, y, dims, preferred_element_type=F32)

    def flat(x):
        return x.reshape(tokens, HD)

    def attend(h):
        dk_acc[h] = jnp.zeros(dk_acc.shape[1:], F32)
        dv_acc[h] = jnp.zeros(dv_acc.shape[1:], F32)

        @pl.loop(0, 4)
        def _(i):
            q = flat(qg[h, i])
            g = flat(gg[h, i])
            keys = [(0, 0), (0, 1), (0, 2), (0, 3), (1, lax.rem(i + ahead, 4)), (2, lax.rem(i + behind, 4))]
            top = None
            for j, (nb, s) in enumerate(keys):
                js = pl.ds(j * tokens, tokens)
                score = dot(q, flat(kk[h, nb, s]), nt)
                bias = bias_g[i, :, js]
                parts = [score[b * BLOCK:(b + 1) * BLOCK] + bias[b:b + 1] for b in range(tokens // BLOCK)]
                score = jnp.concatenate(parts, axis=0)
                s_sc[:, js] = score
                peak = jnp.max(score, axis=1, keepdims=True)
                top = peak if top is None else jnp.maximum(top, peak)
            total = jnp.zeros((tokens, 1), F32)
            out = jnp.zeros((tokens, HD), F32)
            for j, (nb, s) in enumerate(keys):
                js = pl.ds(j * tokens, tokens)
                prob = jnp.exp2((s_sc[:, js] - top) * (SCALE * LOG2E))
                s_sc[:, js] = prob
                total = total + jnp.sum(prob, axis=1, keepdims=True)
                out = out + dot(prob.astype(BF16), flat(vv[h, nb, s]), nn)
            inv = 1.0 / total
            out = out * inv
            res[0, h, i] = out.astype(BF16).reshape(tx, ty, HD)
            grad_dot = jnp.sum(g.astype(F32) * out, axis=1, keepdims=True)
            dq = jnp.zeros((tokens, HD), F32)
            for j, (nb, s) in enumerate(keys):
                js = pl.ds(j * tokens, tokens)
                prob_grad = dot(g, flat(vv[h, nb, s]), nt)
                prob = s_sc[:, js] * inv
                score_grad = (prob * (prob_grad - grad_dot)).astype(BF16)
                dq = dq + dot(score_grad, flat(kk[h, nb, s]), nn)
                dk = dot(score_grad, q, tn)
                dv = dot(prob.astype(BF16), g, tn)
                if nb == 0:
                    dk_acc[h, s] += dk
                    dv_acc[h, s] += dv
                else:
                    part_send[0, h, nb - 1, s] = dk.astype(BF16).reshape(tx, ty, HD)
                    part_send[1, h, nb - 1, s] = dv.astype(BF16).reshape(tx, ty, HD)
            res[1, h, i] = (dq * SCALE).astype(BF16).reshape(tx, ty, HD)

    back = {0: [], 1: [], 2: [], 3: []}

    def give_back(a, h):
        for d in order:
            target = lax.rem(slot + d, 4)
            back[a].append(send(res.at[a, h, target], ret.at[a, slot * hp + h], far(d)))

    parts = {}

    def work(h):
        for d in order:
            for a in (2, 3):
                incoming[h, a, d].wait_recv()
        for a in range(2):
            for d in range(4):
                for nb in (1, 2):
                    forwards[h, a, d, nb].wait_recv()
        if h:
            finish(h - 1)
        attend(h)
        parts[h] = [
            send(part_send.at[a, h, nb], part_recv.at[a, h, nb], (next_group, prev_group)[nb])
            for a in range(2) for nb in range(2)
        ]
        for a in (0, 1):
            give_back(a, h)

    def finish(h):
        for copy in parts[h]:
            copy.wait_recv()
        for a, acc in enumerate((dk_acc, dv_acc)):
            for s in range(4):
                value = acc[h, s] + flat(part_recv[a, h, 0, s]).astype(F32) + flat(part_recv[a, h, 1, s]).astype(F32)
                if a == 0:
                    value = value * SCALE
                res[2 + a, h, s] = value.astype(BF16).reshape(tx, ty, HD)
            give_back(2 + a, h)

    for h in range(hp):
        work(h)
    finish(hp - 1)
    outputs = (o_ref, dq_ref, dk_ref, dv_ref)
    for a in range(4):
        for h in range(hp):
            ret[a, slot * hp + h] = res[a, h, slot]
        for copy in back[a]:
            copy.wait_recv()
        for c in range(heads):
            cols = pl.ds(c * HD, HD)
            if a in (0, 3):
                outputs[a][:, :, cols] = (ret[a, c].astype(F32) + conv[a // 3, :, :, cols]).astype(BF16)
            else:
                outputs[a][:, :, cols] = ret[a, c]
    for copy in sent:
        copy.wait_send()
    for copy, sends, _ in edge_copies:
        pl.when(sends)(copy.wait_send)


def bias_rows(block_pairs, n, tokens):
    quarter = n // 4
    own = lax.axis_index("gx")
    rank = own % quarter
    blocks = tokens // BLOCK
    tiles = jnp.concatenate([
        rank + quarter * jnp.arange(4, dtype=jnp.int32),
        jnp.stack([(own + 1) % n, (own + n - 1) % n]).astype(jnp.int32),
    ])
    key_at = jnp.repeat(tiles, tokens) * blocks + jnp.tile(jnp.arange(tokens, dtype=jnp.int32) // BLOCK, 6)
    query = jnp.arange(8, dtype=jnp.int32)
    pairs = block_pairs[0, 0]
    listed = (pairs[:, 0][:, None, None] == query[None, :, None]) & (pairs[:, 1][:, None, None] == key_at[None, None, :])
    allowed = jnp.any(listed, axis=0) | ((own * blocks + query)[:, None] == key_at[None, :])
    return jnp.where(allowed, 0.0, NEG).astype(F32)


def per_device(n, m, queries, key_tokens, value_tokens, out_grad, conv_weight, block_pairs):
    tx, ty, width = queries.shape
    heads = width // HD
    hp = heads // 4
    tokens = tx * ty
    bias = bias_rows(block_pairs, n, tokens)
    vmem = pl.BlockSpec(memory_space=pltpu.VMEM)
    shape = jax.ShapeDtypeStruct(queries.shape, BF16)
    return pl.pallas_call(
        functools.partial(kernel, n, m, tx, ty),
        out_shape=(shape,) * 4,
        in_specs=[vmem] * 6,
        out_specs=(vmem,) * 4,
        scratch_shapes=[
            pltpu.VMEM((hp, 4, tx, ty, HD), BF16),
            pltpu.VMEM((hp, 4, tx, ty, HD), BF16),
            pltpu.VMEM((hp, 3, 4, tx, ty, HD), BF16),
            pltpu.VMEM((hp, 3, 4, tx, ty, HD), BF16),
            pltpu.VMEM((4, 8, 6 * tokens), F32),
            pltpu.VMEM((tokens, 6 * tokens), F32),
            pltpu.VMEM((hp, 4, tokens, HD), F32),
            pltpu.VMEM((hp, 4, tokens, HD), F32),
            pltpu.VMEM((2, hp, 2, 4, tx, ty, HD), BF16),
            pltpu.VMEM((2, hp, 2, 4, tx, ty, HD), BF16),
            pltpu.VMEM((4, hp, 4, tx, ty, HD), BF16),
            pltpu.VMEM((4, heads, tx, ty, HD), BF16),
            pltpu.VMEM((2, 2, ty, width), BF16),
            pltpu.VMEM((2, 2, tx + 2, 16, width), BF16),
            pltpu.VMEM((2, tx, ty, width), F32),
            pltpu.SemaphoreType.DMA((160,)),
            pltpu.SemaphoreType.DMA((160,)),
            pltpu.SemaphoreType.DMA((4 * hp + 1,)),
        ],
        compiler_params=pltpu.CompilerParams(
            collective_id=0, has_side_effects=True, vmem_limit_bytes=60 * 1024 * 1024
        ),
    )(queries, key_tokens, value_tokens, out_grad, conv_weight, bias)


def solution(mesh):
    grid = P("gx", "gy", None)
    return jax.shard_map(
        functools.partial(per_device, mesh.shape["gx"], mesh.shape["gy"]),
        mesh=mesh,
        in_specs=(grid, grid, grid, grid, P(), P("gx", "gy", None, None)),
        out_specs=(grid, grid, grid, grid),
        check_vma=False,
    )
```

```python
import functools
import math

import jax
import jax.numpy as jnp
from jax import lax
from jax.experimental import pallas as pl
from jax.experimental.pallas import tpu as pltpu
from jax.sharding import PartitionSpec as P

HD = 128
BLOCK = 128
NEG = -1e30
MESH = pl.DeviceIdType.MESH
SCALE = 1.0 / math.sqrt(HD)
LOG2E = math.log2(math.e)
F32 = jnp.float32
BF16 = jnp.bfloat16


def kernel(
    n, m, tx, ty,
    q_ref, k_ref, v_ref, g_ref, w_ref, bias_ref,
    o_ref, dq_ref, dk_ref, dv_ref,
    qg, gg, kk, vv, bias_g, s_sc, dk_acc, dv_acc,
    part_send, part_recv, res, ret, edge, slab, conv,
    send_sem, recv_sem, local_sem,
):
    tokens = tx * ty
    heads = q_ref.shape[2] // HD
    hp = heads // 4
    quarter = n // 4
    own = lax.axis_index("gx")
    col = lax.axis_index("gy")
    slot = own // quarter
    rank = lax.rem(own, quarter)

    def far(d):
        return {"gx": lax.rem(own + d * quarter, n)}

    next_group = {"gx": slot * quarter + lax.rem(rank + 1, quarter)}
    prev_group = {"gx": slot * quarter + lax.rem(rank + quarter - 1, quarter)}
    next_tile = {"gx": lax.rem(own + 1, n)}
    prev_tile = {"gx": lax.rem(own + n - 1, n)}
    next_col = {"gy": lax.rem(col + 1, m)}
    prev_col = {"gy": lax.rem(col + m - 1, m)}

    barrier = pltpu.get_barrier_semaphore()
    partners = [far(1), far(2), far(3), next_group, prev_group, next_tile, prev_tile, next_col, prev_col]
    for partner in partners:
        pl.semaphore_signal(barrier, inc=1, device_id=partner, device_id_type=MESH)
    pl.semaphore_wait(barrier, len(partners))

    count = [0]
    sent = []

    def send(src, dst, device):
        at = count[0]
        count[0] += 1
        copy = pltpu.make_async_remote_copy(
            src_ref=src, dst_ref=dst, send_sem=send_sem.at[at], recv_sem=recv_sem.at[at],
            device_id=device, device_id_type=MESH,
        )
        copy.start()
        sent.append(copy)
        return copy

    edge_copies = []

    def edge_send(src, dst, device, sends, receives):
        at = count[0]
        count[0] += 1
        copy = pltpu.make_async_remote_copy(
            src_ref=src, dst_ref=dst, send_sem=send_sem.at[at], recv_sem=recv_sem.at[at],
            device_id=device, device_id_type=MESH,
        )

        @pl.when(sends)
        def _():
            copy.start()

        @pl.when(jnp.logical_not(receives))
        def _():
            dst[...] = jnp.zeros(dst.shape, BF16)

        edge_copies.append((copy, sends, receives))

    def head_cols(head):
        return pl.ds(pl.multiple_of(head * HD, HD), HD)

    order = (2, 1, 3)
    arrays = ((k_ref, lambda h, s: kk.at[h, 0, s]), (v_ref, lambda h, s: vv.at[h, 0, s]),
              (q_ref, lambda h, s: qg.at[h, s]), (g_ref, lambda h, s: gg.at[h, s]))
    incoming = {}
    locals_ = []
    for h in range(hp):
        for a, (ref, place) in enumerate(arrays):
            for d in order:
                target = lax.rem(slot + d, 4)
                incoming[h, a, d] = send(ref.at[:, :, head_cols(target * hp + h)], place(h, slot), far(d))
            mine = pltpu.make_async_copy(
                ref.at[:, :, head_cols(slot * hp + h)], place(h, slot), local_sem.at[h * 4 + a])
            mine.start()
            locals_.append(mine)
        if h == 0:
            for a, ref in enumerate((v_ref, g_ref)):
                edge_send(ref.at[pl.ds(tx - 1, 1)], edge.at[a, pl.ds(0, 1)], next_tile, own < n - 1, own > 0)
                edge_send(ref.at[pl.ds(0, 1)], edge.at[a, pl.ds(1, 1)], prev_tile, own > 0, own < n - 1)
            bias_copies = [send(bias_ref, bias_g.at[slot], far(d)) for d in order]
            mine = pltpu.make_async_copy(bias_ref, bias_g.at[slot], local_sem.at[hp * 4])
            mine.start()
            locals_.append(mine)
    slab_copies = []
    for a, ref in enumerate((v_ref, g_ref)):
        slab_copies.append(send(ref.at[:, pl.ds(ty - 16, 16)], slab.at[a, 0, pl.ds(1, tx)], next_col))
        slab_copies.append(send(ref.at[:, pl.ds(0, 16)], slab.at[a, 1, pl.ds(1, tx)], prev_col))
    for mine in locals_:
        mine.wait()

    forwards = {}

    def forward(h, d):
        s = lax.rem(slot + 4 - d, 4)
        for a, buf in enumerate((kk, vv)):
            if d:
                incoming[h, a, d].wait_recv()
            forwards[h, a, d, 1] = send(buf.at[h, 0, s], buf.at[h, 1, s], prev_group)
            forwards[h, a, d, 2] = send(buf.at[h, 0, s], buf.at[h, 2, s], next_group)

    for h in range(hp):
        forward(h, 0)
    for copy, _, receives in edge_copies:
        pl.when(receives)(copy.wait_recv)
    for a in range(2):
        for x, e in ((0, 0), (tx + 1, 1)):
            slab_copies.append(send(edge.at[a, pl.ds(e, 1), pl.ds(ty - 16, 16)], slab.at[a, 0, pl.ds(x, 1)], next_col))
            slab_copies.append(send(edge.at[a, pl.ds(e, 1), pl.ds(0, 16)], slab.at[a, 1, pl.ds(x, 1)], prev_col))
    for d in (1, 3, 2):
        forward(0, d)

    for copy in slab_copies:
        copy.wait_recv()
    has_up = (own > 0).astype(F32)
    has_down = (own < n - 1).astype(F32)
    has_left = (col > 0).astype(F32)
    has_right = (col < m - 1).astype(F32)
    for a, ref in enumerate((v_ref, g_ref)):

        @pl.loop(0, heads)
        def _(c, a=a, ref=ref):
            cols = head_cols(c)
            row_id = lax.broadcasted_iota(jnp.int32, (ty, HD), 0)
            sums = [None] * tx
            for x in range(tx + 2):
                if x == 0:
                    row = edge[a, 0, :, cols].astype(F32) * has_up
                elif x == tx + 1:
                    row = edge[a, 1, :, cols].astype(F32) * has_down
                else:
                    row = ref[x - 1, :, cols].astype(F32)
                left = slab[a, 0, x, :, cols].astype(F32)[15:16] * has_left
                right = slab[a, 1, x, :, cols].astype(F32)[0:1] * has_right
                if x == 0:
                    left, right = left * has_up, right * has_up
                if x == tx + 1:
                    left, right = left * has_down, right * has_down
                shifted = (
                    jnp.where(row_id == 0, left, pltpu.roll(row, 1, 0)),
                    row,
                    jnp.where(row_id == ty - 1, right, pltpu.roll(row, ty - 1, 0)),
                )
                for step in (-1, 0, 1):
                    target = x - 1 - step
                    if 0 <= target < tx:
                        for b in range(3):
                            tap = 3 * (step + 1) + b
                            tap = tap if a == 0 else 8 - tap
                            term = w_ref[pl.ds(tap, 1), cols] * shifted[b]
                            sums[target] = term if sums[target] is None else sums[target] + term
            for x in range(tx):
                conv[a, x, :, cols] = sums[x]

    for h in range(1, hp):
        for d in (1, 3, 2):
            forward(h, d)
    for copy in bias_copies:
        copy.wait_recv()

    ahead = (rank == quarter - 1).astype(jnp.int32)
    behind = 3 * (rank == 0).astype(jnp.int32)
    nt = (((1,), (1,)), ((), ()))
    nn = (((1,), (0,)), ((), ()))
    tn = (((0,), (0,)), ((), ()))

    def dot(x, y, dims):
        return lax.dot_general(x, y, dims, preferred_element_type=F32)

    def flat(x):
        return x.reshape(tokens, HD)

    def attend(h, first, last):
        if first == 0:
            dk_acc[h] = jnp.zeros(dk_acc.shape[1:], F32)
            dv_acc[h] = jnp.zeros(dv_acc.shape[1:], F32)

        @pl.loop(first, last)
        def _(i):
            q = flat(qg[h, i])
            g = flat(gg[h, i])
            keys = [(0, 0), (0, 1), (0, 2), (0, 3), (1, lax.rem(i + ahead, 4)), (2, lax.rem(i + behind, 4))]
            top = None
            for j, (nb, s) in enumerate(keys):
                js = pl.ds(j * tokens, tokens)
                score = dot(q, flat(kk[h, nb, s]), nt)
                bias = bias_g[i, :, js]
                parts = [score[b * BLOCK:(b + 1) * BLOCK] + bias[b:b + 1] for b in range(tokens // BLOCK)]
                score = jnp.concatenate(parts, axis=0)
                s_sc[:, js] = score
                peak = jnp.max(score, axis=1, keepdims=True)
                top = peak if top is None else jnp.maximum(top, peak)
            total = jnp.zeros((tokens, 1), F32)
            out = jnp.zeros((tokens, HD), F32)
            for j, (nb, s) in enumerate(keys):
                js = pl.ds(j * tokens, tokens)
                prob = jnp.exp2((s_sc[:, js] - top) * (SCALE * LOG2E))
                s_sc[:, js] = prob
                total = total + jnp.sum(prob, axis=1, keepdims=True)
                out = out + dot(prob.astype(BF16), flat(vv[h, nb, s]), nn)
            inv = 1.0 / total
            out = out * inv
            res[0, h, i] = out.astype(BF16).reshape(tx, ty, HD)
            grad_dot = jnp.sum(g.astype(F32) * out, axis=1, keepdims=True)
            dq = jnp.zeros((tokens, HD), F32)
            for j, (nb, s) in enumerate(keys):
                js = pl.ds(j * tokens, tokens)
                prob_grad = dot(g, flat(vv[h, nb, s]), nt)
                prob = s_sc[:, js] * inv
                score_grad = (prob * (prob_grad - grad_dot)).astype(BF16)
                dq = dq + dot(score_grad, flat(kk[h, nb, s]), nn)
                dk = dot(score_grad, q, tn)
                dv = dot(prob.astype(BF16), g, tn)
                if nb == 0:
                    dk_acc[h, s] += dk
                    dv_acc[h, s] += dv
                else:
                    part_send[0, h, nb - 1, s] = dk.astype(BF16).reshape(tx, ty, HD)
                    part_send[1, h, nb - 1, s] = dv.astype(BF16).reshape(tx, ty, HD)
            res[1, h, i] = (dq * SCALE).astype(BF16).reshape(tx, ty, HD)

    back = {0: [], 1: [], 2: [], 3: []}

    def give_back(a, h):
        for d in order:
            target = lax.rem(slot + d, 4)
            back[a].append(send(res.at[a, h, target], ret.at[a, slot * hp + h], far(d)))

    parts = {}

    def work(h):
        for d in order:
            for a in (2, 3):
                incoming[h, a, d].wait_recv()
        for a in range(2):
            for d in range(4):
                for nb in (1, 2):
                    forwards[h, a, d, nb].wait_recv()
        if h:
            finish(h - 1)
        parts[h] = {0: [], 1: []}
        width = 4 if h < hp - 1 else 2
        for first in range(0, 4, width):
            attend(h, first, first + width)
            for a in range(2):
                for i in range(first, first + width):
                    for nb, shift in ((0, ahead), (1, behind)):
                        at = (a, h, nb, lax.rem(i + shift, 4))
                        parts[h][a].append(
                            send(part_send.at[at], part_recv.at[at], (next_group, prev_group)[nb]))
        for a in (0, 1):
            give_back(a, h)

    def finish(h):
        for a, acc in enumerate((dk_acc, dv_acc)):
            for copy in parts[h][a]:
                copy.wait_recv()
            for s in range(4):
                value = acc[h, s] + flat(part_recv[a, h, 0, s]).astype(F32) + flat(part_recv[a, h, 1, s]).astype(F32)
                if a == 0:
                    value = value * SCALE
                res[2 + a, h, s] = value.astype(BF16).reshape(tx, ty, HD)
            give_back(2 + a, h)

    for h in range(hp):
        work(h)
    finish(hp - 1)
    outputs = (o_ref, dq_ref, dk_ref, dv_ref)
    for a in range(4):
        for h in range(hp):
            ret[a, slot * hp + h] = res[a, h, slot]
        for copy in back[a]:
            copy.wait_recv()
        for c in range(heads):
            cols = pl.ds(c * HD, HD)
            if a in (0, 3):
                outputs[a][:, :, cols] = (ret[a, c].astype(F32) + conv[a // 3, :, :, cols]).astype(BF16)
            else:
                outputs[a][:, :, cols] = ret[a, c]
    for copy in sent:
        copy.wait_send()
    for copy, sends, _ in edge_copies:
        pl.when(sends)(copy.wait_send)


def bias_rows(block_pairs, n, tokens):
    quarter = n // 4
    own = lax.axis_index("gx")
    rank = own % quarter
    blocks = tokens // BLOCK
    tiles = jnp.concatenate([
        rank + quarter * jnp.arange(4, dtype=jnp.int32),
        jnp.stack([(own + 1) % n, (own + n - 1) % n]).astype(jnp.int32),
    ])
    key_at = jnp.repeat(tiles, tokens) * blocks + jnp.tile(jnp.arange(tokens, dtype=jnp.int32) // BLOCK, 6)
    query = jnp.arange(8, dtype=jnp.int32)
    pairs = block_pairs[0, 0]
    listed = (pairs[:, 0][:, None, None] == query[None, :, None]) & (pairs[:, 1][:, None, None] == key_at[None, None, :])
    allowed = jnp.any(listed, axis=0) | ((own * blocks + query)[:, None] == key_at[None, :])
    return jnp.where(allowed, 0.0, NEG).astype(F32)


def per_device(n, m, queries, key_tokens, value_tokens, out_grad, conv_weight, block_pairs):
    tx, ty, width = queries.shape
    heads = width // HD
    hp = heads // 4
    tokens = tx * ty
    bias = bias_rows(block_pairs, n, tokens)
    vmem = pl.BlockSpec(memory_space=pltpu.VMEM)
    shape = jax.ShapeDtypeStruct(queries.shape, BF16)
    return pl.pallas_call(
        functools.partial(kernel, n, m, tx, ty),
        out_shape=(shape,) * 4,
        in_specs=[vmem] * 6,
        out_specs=(vmem,) * 4,
        scratch_shapes=[
            pltpu.VMEM((hp, 4, tx, ty, HD), BF16),
            pltpu.VMEM((hp, 4, tx, ty, HD), BF16),
            pltpu.VMEM((hp, 3, 4, tx, ty, HD), BF16),
            pltpu.VMEM((hp, 3, 4, tx, ty, HD), BF16),
            pltpu.VMEM((4, 8, 6 * tokens), F32),
            pltpu.VMEM((tokens, 6 * tokens), F32),
            pltpu.VMEM((hp, 4, tokens, HD), F32),
            pltpu.VMEM((hp, 4, tokens, HD), F32),
            pltpu.VMEM((2, hp, 2, 4, tx, ty, HD), BF16),
            pltpu.VMEM((2, hp, 2, 4, tx, ty, HD), BF16),
            pltpu.VMEM((4, hp, 4, tx, ty, HD), BF16),
            pltpu.VMEM((4, heads, tx, ty, HD), BF16),
            pltpu.VMEM((2, 2, ty, width), BF16),
            pltpu.VMEM((2, 2, tx + 2, 16, width), BF16),
            pltpu.VMEM((2, tx, ty, width), F32),
            pltpu.SemaphoreType.DMA((160,)),
            pltpu.SemaphoreType.DMA((160,)),
            pltpu.SemaphoreType.DMA((4 * hp + 1,)),
        ],
        compiler_params=pltpu.CompilerParams(
            collective_id=0, has_side_effects=True, vmem_limit_bytes=60 * 1024 * 1024
        ),
    )(queries, key_tokens, value_tokens, out_grad, conv_weight, bias)


def solution(mesh):
    grid = P("gx", "gy", None)
    return jax.shard_map(
        functools.partial(per_device, mesh.shape["gx"], mesh.shape["gy"]),
        mesh=mesh,
        in_specs=(grid, grid, grid, grid, P(), P("gx", "gy", None, None)),
        out_specs=(grid, grid, grid, grid),
        check_vma=False,
    )
```
